32 devices in a mesh: member: 2 (over x), tm: 4 (over z), tile: 4 (over y, core).
Axes of the slice: x: 2, y: 2, z: 4, core: 2. Of those that a mesh axis runs over, the one named last changes fastest.
Arguments:
- flux: bfloat16 [64, 32, 16384], P(('member', 'tm'), 'tile'), parts along dimension 0, may hold values from -6 to 6
- footprint: bfloat16 [4, 256, 4, 16384], P('tm', 'tile'), may hold values from 1.4424324e-05 to 0.014404297
- foot_slot: int32 [4, 256, 4], P('tm', 'tile'), may hold values from 0 to 7
- wanted: int32 [4, 4, 4, 2], P('tm', 'tile'), may hold values from 0 to 127
- counts: int32 [4, 4, 4], P('tm', 'tile'), may hold values from 1 to 2
- observed: float32 [4, 256], P('tm', 'tile'), may hold values from -6 to 6
- inv_var: float32 [4, 256], P('tm', 'tile'), may hold values from 25.6 to 102.4
Outputs:
- modeled: float32 [8, 256], P(('member', 'tm'), 'tile'), parts along dimension 0
- gradient: float32 [64, 32, 16384], P(('member', 'tm'), 'tile'), parts along dimension 0
The draws below stay inside these ranges and needn't reach their ends.
There are 2 independent parts, one for each index of `member`. The reference program is written for one: setup_inputs(seed, part) draws one part's arguments, and reference() takes and returns one part's arrays. A program takes and returns all parts, laid end to end along the dimension named above; an argument that names none is the same for every part. Nothing has to cross between parts.
All inputs are finite; a program needn't handle non-finite values.
Results may differ from the reference program's by a relative error of at most 0.0042.
Values may be sent and summed in bfloat16 or wider, within the bound.
No kernel may reach another device: no remote copies, remote signals or barrier semaphores. Data moves between devices by JAX's collectives and lax.ppermute only.
A program may use at most 128 MiB of HBM per device.

```python
import math
import jax
import jax.numpy as jnp
import numpy as np
from jax import lax

TILE_CELLS = 16384
TW = 8
TILES_DEV = 8
NS = 64
K = 4
CAP = 2
TIMES = 32
TILES = 32
SOUNDINGS = 256
N_TM = 4
N_TILE = 4


def with_ends(drawn, own_key, least, largest):
    index_at = [jax.random.randint(jax.random.fold_in(own_key, axis), (), 0, length) for axis, length in enumerate(drawn.shape)]
    widest = drawn.shape.index(max(drawn.shape))
    beside = index_at[:widest] + [(index_at[widest] + 1) % drawn.shape[widest]] + index_at[widest + 1:]
    return drawn.at[tuple(index_at)].set(least).at[tuple(beside)].set(largest)


def level_of(own_key, extent, cuts, least, top_value):
    gain, own = 1.0, jax.random.fold_in(own_key, 6)
    for dim, parts in cuts:
        heights = jnp.exp(jax.random.uniform(jax.random.fold_in(own, dim), (parts,), jnp.float32, least / len(cuts), top_value / len(cuts)))
        gain = gain * jnp.repeat(heights, extent[dim] // parts).reshape([-1 if axis == dim else 1 for axis in range(len(extent))])
    return gain


def cumulative_ranks(amount, skew):
    weights = [(1 << 20) // math.isqrt(grade ** skew) + 1 for grade in range(1, amount + 1)]
    width = 1 + sum(weights) // (1 << 30)
    return np.cumsum(np.array([max(1, weight // width) for weight in weights]))


def ranked_ids(stream_key, dims, count, lean):
    grid = cumulative_ranks(count, lean)
    pick = jax.random.randint(jax.random.fold_in(stream_key, 1), dims, 0, int(grid[count - 1]))
    standing = jnp.searchsorted(jnp.asarray(grid, jnp.int32), pick, side="right")
    return jax.random.permutation(jax.random.fold_in(stream_key, 2), count)[standing].astype(jnp.int32)


def noise(stream_key, shape, width, limit, pieces=(), kind=jnp.bfloat16):
    loudness = level_of(stream_key, shape, pieces, -0.22, 0.18) if pieces else 1.0
    entries = jax.random.normal(stream_key, shape, jnp.float32) * width * loudness
    return jnp.minimum(jnp.maximum(entries, -limit), limit).astype(kind)


def setup_inputs(seed: int = 0, part: int = 0) -> dict:
    arg_keys = jax.random.split(jax.random.key(seed), 8)
    own_keys = jax.random.split(jax.random.fold_in(arg_keys[7], part), 8)
    return {
        "flux": noise(own_keys[0], (TIMES, TILES, TILE_CELLS), 1.0, 6.0, ((0, 4), (1, 4))),
        "footprint": jnp.clip(jnp.exp(math.log(0.014404297) - 6.906366 * jax.random.uniform(arg_keys[1], (N_TM, SOUNDINGS, K, TILE_CELLS), jnp.float32) ** level_of(arg_keys[1], (N_TM, SOUNDINGS, K, TILE_CELLS), ((0, 4), (1, 4)), -0.2, 0.2)), 1.4424324035644531e-05, 0.014404297).astype(jnp.bfloat16),
        "foot_slot": with_ends(ranked_ids(arg_keys[2], (N_TM, SOUNDINGS, K), N_TILE * CAP, 2), jax.random.fold_in(arg_keys[2], 3), 0, (N_TILE * CAP) - 1).astype(jnp.int32),
        "wanted": with_ends(jax.random.randint(arg_keys[3], (N_TM, N_TILE, N_TILE, CAP), 0, 2 * TW * TILES_DEV), jax.random.fold_in(arg_keys[3], 1), 0, (2 * TW * TILES_DEV) - 1).astype(jnp.int32),
        "counts": with_ends(jax.random.randint(arg_keys[4], (N_TM, N_TILE, N_TILE), 1, CAP + 1), jax.random.fold_in(arg_keys[4], 1), 1, CAP).astype(jnp.int32),
        "observed": noise(arg_keys[5], (N_TM, SOUNDINGS), 1.0, 6.0, ((0, 4), (1, 4)), jnp.float32),
        "inv_var": jnp.clip(jnp.exp(math.log(102.4) - 1.3862944 * jax.random.uniform(arg_keys[6], (N_TM, SOUNDINGS), jnp.float32) ** level_of(arg_keys[6], (N_TM, SOUNDINGS), ((0, 4), (1, 4)), -0.2, 0.2)), 25.6, 102.4),
    }


def reference(flux, footprint, foot_slot, wanted, counts, observed, inv_var):
    times, tiles, cells = flux.shape
    padded = jnp.concatenate([jnp.zeros((TW, tiles, cells), flux.dtype), flux], 0)
    owner_of = (jnp.arange(SOUNDINGS, dtype=jnp.int32) // NS).astype(jnp.int32)

    def window(grad, items):
        index, prints, entry, asked, have, measured, precision_w = items
        peer = entry // CAP
        place = entry % CAP
        asked_flat = asked.reshape(N_TILE, N_TILE * CAP)
        row = asked_flat[owner_of[:, None], entry]
        livef = (place < have[owner_of[:, None], peer]).astype(jnp.float32)
        step = (index * TW + row // TILES_DEV).astype(jnp.int32)
        tile = (peer * TILES_DEV + row % TILES_DEV).astype(jnp.int32)
        values = padded[step, tile].astype(jnp.float32)
        prints_f = prints.astype(jnp.float32)
        modeled = jnp.sum(livef[:, :, None] * prints_f * values, axis=(1, 2))
        coef = ((modeled - measured) * precision_w).astype(jnp.bfloat16)
        coef = lax.optimization_barrier(coef).astype(jnp.float32)
        contrib = prints_f * (coef[:, None] * livef)[:, :, None]
        grad = grad.at[step, tile].add(contrib)
        return grad, modeled

    start = jnp.zeros((times + TW, tiles, cells), jnp.float32)
    windows = jnp.arange(N_TM, dtype=jnp.int32)
    grad, modeled = lax.scan(window, start, (windows, footprint, foot_slot, wanted, counts, observed, inv_var))
    return modeled, grad[TW:]
```

```python
import functools

import jax
import jax.numpy as jnp
from jax import lax
from jax.experimental import pallas as pl
from jax.experimental.pallas import tpu as pltpu
from jax.sharding import PartitionSpec as P


VMEM = pl.BlockSpec(memory_space=pltpu.VMEM)
HBM = pl.BlockSpec(memory_space=pltpu.HBM)
MIB = 1 << 20


def passed_along(value, steps):
    count = lax.axis_size("tm")
    first, last = (max(0, -steps), min(count, count - steps))
    return lax.ppermute(value, "tm", [(source, source + steps) for source in range(first, last)])


def swapped(value, mask):
    return lax.ppermute(value, "tile", [(j, j ^ mask) for j in range(lax.axis_size("tile"))])


def chunks_of(cells, width):
    width = min(width, cells)
    return [(start, width) for start in range(0, cells, width)]


def footprint_kernel(footprint, out, sem):
    soundings, per, cells = footprint.shape
    copy = pltpu.make_async_copy(footprint.reshape(soundings * per, cells), out, sem)
    copy.start()
    copy.wait()


def gather_kernel(owners, capacity, *refs):
    tables, own = refs[:owners], refs[owners]
    later, now, placing = refs[owners + 1 : 2 * owners + 1], refs[2 * owners + 1 : 3 * owners + 1], refs[3 * owners + 1]
    own_rows, cells = own.shape
    slots = owners * capacity
    me = lax.axis_index("tile")
    mine = pl.ds(me * capacity, capacity)
    ids = [t[1, mine, :] for t in tables] + [t[0, mine, :] - own_rows for t in tables]
    ids = jnp.concatenate(ids, axis=0)
    place = (ids == lax.broadcasted_iota(jnp.int32, ids.shape, 1)).astype(jnp.float32).astype(jnp.bfloat16)
    placing[...] = place
    for start, width in chunks_of(cells, 2048):
        at = pl.ds(start, width)
        rows = jnp.dot(place, own[:, at], preferred_element_type=jnp.float32).astype(jnp.bfloat16)
        for p in range(owners):
            later[p][:, at] = rows[p * capacity : (p + 1) * capacity]
            now[p][:, at] = rows[slots + p * capacity : slots + (p + 1) * capacity]


def adjoint_kernel(owners, capacity, per, *refs):
    prints, entry, slot_of, observed, inv_var = refs[:5]
    first = refs[5:7]
    arrived = refs[7 : 6 + owners]
    modeled, adjoint = refs[6 + owners], refs[7 + owners : 7 + 2 * owners]
    entries, cells = prints.shape
    soundings = entries // per
    slots = owners * capacity
    scores = jnp.zeros((slots, entries), jnp.float32)
    for start, width in chunks_of(cells, 2048):
        at = pl.ds(start, width)
        rows = [first[0][:, at] + first[1][:, at]] + [a[:, at] for a in arrived]
        rows = jnp.concatenate(rows, axis=0)
        scores += lax.dot_general(rows, prints[:, at], (((1,), (1,)), ((), ())), preferred_element_type=jnp.float32)
    select = entry[...] == slot_of[...]
    entry_sums = jnp.sum(jnp.where(select, scores, 0.0), axis=0, keepdims=True)
    group = lax.broadcasted_iota(jnp.int32, (entries, soundings), 0) // per
    member = group == lax.broadcasted_iota(jnp.int32, (entries, soundings), 1)
    sums = lax.dot_general(
        jnp.broadcast_to(entry_sums, (8, entries)),
        member.astype(jnp.float32),
        (((1,), (0,)), ((), ())),
        precision=lax.Precision.HIGHEST,
        preferred_element_type=jnp.float32,
    )
    modeled[...] = sums[:1]
    coef = ((sums - observed[...]) * inv_var[...]).astype(jnp.bfloat16)
    spread = lax.dot_general(
        coef, member.astype(jnp.float32).astype(jnp.bfloat16), (((1,), (1,)), ((), ())), preferred_element_type=jnp.float32
    )
    spread = jnp.where(select, spread[:1], 0.0).astype(jnp.bfloat16)
    for start, width in chunks_of(cells, 2048):
        at = pl.ds(start, width)
        back = jnp.dot(spread, prints[:, at], preferred_element_type=jnp.float32).astype(jnp.bfloat16)
        for p in range(owners):
            adjoint[p][:, at] = back[p * capacity : (p + 1) * capacity]


def placing_kernel(*refs):
    placing, returned, out, held, sems = refs[0], refs[1:-3], refs[-3], refs[-2], refs[-1]
    place = placing[...]
    copies = []
    for n, (start, width) in enumerate(chunks_of(held.shape[1], held.shape[1] // 8)):
        at = pl.ds(start, width)
        rows = jnp.concatenate([r[:, at] for r in returned], axis=0)
        held[:, at] = lax.dot_general(place, rows, (((0,), (0,)), ((), ())), preferred_element_type=jnp.float32)
        copies.append(pltpu.make_async_copy(held.at[:, at], out.at[:, at], sems.at[n]))
        copies[-1].start()
    for copy in copies:
        copy.wait()


def on_device(flux, footprint, foot_slot, wanted, counts, observed, inv_var):
    steps_win, tiles_dev, cells = flux.shape
    owners = lax.axis_size("tile")
    capacity = wanted.shape[3]
    slots = owners * capacity
    own_rows = steps_win * tiles_dev
    soundings, per = foot_slot.shape[1:]
    entries = soundings * per
    me = lax.axis_index("tile")
    half = functools.partial(jax.ShapeDtypeStruct, dtype=jnp.bfloat16)
    params = functools.partial(pltpu.CompilerParams)

    own = flux.reshape(own_rows, cells)
    table = jnp.broadcast_to(wanted.reshape(slots, 1), (slots, own_rows))
    tables = jnp.stack([table, passed_along(table, -1)])
    tables = [tables] + [swapped(tables, p) for p in range(1, owners)]

    block = half((capacity, cells))
    gathered = pl.pallas_call(
        functools.partial(gather_kernel, owners, capacity),
        in_specs=[VMEM] * (owners + 1),
        out_specs=[VMEM] * (2 * owners + 1),
        out_shape=[block] * (2 * owners) + [half((2 * slots, own_rows))],
        compiler_params=params(vmem_limit_bytes=16 * MIB),
        name="gather",
    )(*tables, own)
    later, now, placing = gathered[:owners], gathered[owners:-1], gathered[-1]

    prints = pl.pallas_call(
        footprint_kernel,
        in_specs=[HBM],
        out_specs=VMEM,
        out_shape=half((entries, cells)),
        scratch_shapes=[pltpu.SemaphoreType.DMA],
        compiler_params=params(vmem_limit_bytes=20 * MIB),
        name="prints",
    )(footprint.reshape(soundings, per, cells))

    past = [passed_along(later[p], 1) for p in range(owners - 1, -1, -1)][::-1]
    arrived = [swapped(past[p] + now[p], p) for p in range(owners - 1, 0, -1)][::-1]

    owner_at = jnp.arange(owners, dtype=jnp.int32) ^ me
    have = jnp.sum(jnp.where(owner_at[:, None] == jnp.arange(owners)[None, :], counts.reshape(1, owners), 0), axis=1)
    place = jnp.arange(capacity, dtype=jnp.int32)[None, :]
    slot_of = jnp.where(place < have[:, None], owner_at[:, None] * capacity + place, -1).reshape(slots, 1)

    results = pl.pallas_call(
        functools.partial(adjoint_kernel, owners, capacity, per),
        in_specs=[VMEM] * (6 + owners),
        out_specs=[VMEM] * (1 + owners),
        out_shape=[jax.ShapeDtypeStruct((1, soundings), jnp.float32)] + [block] * owners,
        compiler_params=params(vmem_limit_bytes=24 * MIB),
        name="adjoint",
    )(prints, foot_slot.reshape(1, entries), slot_of, observed, inv_var, past[0], now[0], *arrived)
    modeled, adjoint = results[0], results[1:]

    returned = [adjoint[0]] + [swapped(adjoint[p], p) for p in range(1, owners)]
    incoming = [passed_along(r, -1) for r in returned]

    grad = pl.pallas_call(
        placing_kernel,
        in_specs=[VMEM] * (1 + 2 * owners),
        out_specs=HBM,
        out_shape=jax.ShapeDtypeStruct((own_rows, cells), jnp.float32),
        scratch_shapes=[pltpu.VMEM((own_rows, cells), jnp.float32), pltpu.SemaphoreType.DMA((8,))],
        compiler_params=params(vmem_limit_bytes=20 * MIB),
        name="placing",
    )(placing, *incoming, *returned)
    return (modeled, grad.reshape(steps_win, tiles_dev, cells))


def solution(mesh):
    placed = (
        P(("member", "tm"), "tile", None),
        P("tm", "tile", None, None),
        P("tm", "tile", None),
        P("tm", "tile", None, None),
        P("tm", "tile", None),
        P("tm", "tile"),
        P("tm", "tile"),
    )
    return jax.shard_map(
        on_device,
        mesh=mesh,
        in_specs=placed,
        out_specs=(P(("member", "tm"), "tile"), P(("member", "tm"), "tile", None)),
        check_vma=False,
    )
```

```python
import functools

import jax
import jax.numpy as jnp
from jax import lax
from jax.experimental import pallas as pl
from jax.experimental.pallas import tpu as pltpu
from jax.sharding import PartitionSpec as P


VMEM = pl.BlockSpec(memory_space=pltpu.VMEM)
HBM = pl.BlockSpec(memory_space=pltpu.HBM)
MIB = 1 << 20


def passed_along(value, steps):
    count = lax.axis_size("tm")
    return lax.ppermute(value, "tm", [(source, (source + steps) % count) for source in range(count)])


def swapped(value, mask):
    return lax.ppermute(value, "tile", [(j, j ^ mask) for j in range(lax.axis_size("tile"))])


def in_hbm(value):
    return pltpu.with_memory_space_constraint(value, pltpu.HBM)


def chunks_of(cells, width):
    width = min(width, cells)
    return [(start, width) for start in range(0, cells, width)]


def fetch_kernel(count, start, *refs):
    sources, kept, sems = refs[:count], refs[count : 2 * count], refs[2 * count]
    copies = []
    for n, (source, keep) in enumerate(zip(sources, kept)):
        if source.shape != keep.shape:
            soundings, per, cells = source.shape
            source = source.reshape(soundings * per, cells).at[:, pl.ds(start, keep.shape[1])]
        copies.append(pltpu.make_async_copy(source, keep, sems.at[n]))
        copies[-1].start()
    for copy in copies:
        copy.wait()


def fetched(sources, shapes, start):
    return pl.pallas_call(
        functools.partial(fetch_kernel, len(sources), start),
        in_specs=[HBM] * len(sources),
        out_specs=[VMEM] * len(sources),
        out_shape=[jax.ShapeDtypeStruct(shape, x.dtype) for shape, x in zip(shapes, sources)],
        scratch_shapes=[pltpu.SemaphoreType.DMA((len(sources),))],
        compiler_params=pltpu.CompilerParams(vmem_limit_bytes=12 * MIB),
    )(*[in_hbm(x) for x in sources])


def gather_kernel(owners, capacity, *refs):
    tables, own = refs[:2]
    far, near, now, placing = refs[2], refs[3], refs[4 : 4 + owners], refs[4 + owners]
    own_rows, cells = own.shape
    slots = owners * capacity
    split = owners // 2
    last = lax.axis_index("tm") == lax.axis_size("tm") - 1
    asked = [tables[p, 1] for p in range(owners)] + [tables[p, 0] - own_rows for p in range(owners)]
    asked = jnp.concatenate(asked, axis=0)
    mine = lax.broadcasted_iota(jnp.int32, asked.shape, 1) == lax.axis_index("tile")
    ids = jnp.sum(jnp.where(mine, asked, 0), axis=1, keepdims=True)
    shape = (2 * slots, own_rows)
    ahead = lax.broadcasted_iota(jnp.int32, shape, 0) < jnp.where(last, slots, 0)
    place = one_if((ids == lax.broadcasted_iota(jnp.int32, shape, 1)) & jnp.logical_not(ahead))
    placing[...] = place
    for start, width in chunks_of(cells, cells // 4):
        at = pl.ds(start, width)
        rows = jnp.dot(place, own[:, at], preferred_element_type=jnp.float32).astype(jnp.bfloat16)
        for p in range(owners):
            ahead = rows[p * capacity : (p + 1) * capacity]
            if p < split:
                near[p, :, at] = ahead
            else:
                far[p - split, :, at] = ahead
            now[p][:, at] = rows[slots + p * capacity : slots + (p + 1) * capacity]


def in_parts(value):
    parts, rest = [], value
    for _ in range(3):
        parts.append(rest.astype(jnp.bfloat16).astype(jnp.float32))
        rest = rest - parts[-1]
    return jnp.concatenate(parts + [jnp.zeros((5, value.shape[1]), jnp.float32)], axis=0).astype(jnp.bfloat16)


def spread_by(value, picks, dim):
    parts = lax.dot_general(in_parts(value), picks, (((1,), (dim,)), ((), ())), preferred_element_type=jnp.float32)
    return parts[0:1] + parts[1:2] + parts[2:3]


def one_if(condition):
    return condition.astype(jnp.float32).astype(jnp.bfloat16)


def adjoint_kernel(owners, capacity, per, *refs):
    prints = refs[:2]
    used, counts, observed, inv_var, near, now = refs[2:8]
    arrived = refs[8 : 7 + owners]
    modeled, adjoint = refs[7 + owners], refs[8 + owners : 8 + 2 * owners]
    entries, width = prints[0].shape
    soundings = entries // per
    slots = owners * capacity
    pieces = [(n, start, w) for n in range(len(prints)) for start, w in chunks_of(width, width // 4)]
    shape = (entries, soundings)
    member = one_if(lax.broadcasted_iota(jnp.int32, shape, 0) // per == lax.broadcasted_iota(jnp.int32, shape, 1))
    shape = (entries, entries)
    same = one_if(lax.broadcasted_iota(jnp.int32, shape, 0) // per == lax.broadcasted_iota(jnp.int32, shape, 1) // per)
    measured = spread_by(observed[...], member, 1)
    certain = spread_by(inv_var[...], member, 1)
    entry = jnp.dot(used[...].astype(jnp.float32).astype(jnp.bfloat16), member.T, preferred_element_type=jnp.float32)
    own_entry = lax.broadcasted_iota(jnp.int32, (per, entries), 1) % per == lax.broadcasted_iota(jnp.int32, (per, entries), 0)
    entry = jnp.sum(jnp.where(own_entry, entry, 0.0), axis=0, keepdims=True).astype(jnp.int32)
    slot = lax.broadcasted_iota(jnp.int32, (slots, owners), 0)
    owner, place = (slot // capacity) ^ lax.axis_index("tile"), slot % capacity
    its = owner == lax.broadcasted_iota(jnp.int32, (slots, owners), 1)
    slot_of = jnp.where(its & (place < counts[...]), owner * capacity + place + 1, 0)
    slot_of = jnp.sum(slot_of, axis=1, keepdims=True) - 1
    select = entry == slot_of
    scores = jnp.zeros((slots, entries), jnp.float32)
    for n, start, w in pieces:
        at = pl.ds(n * width + start, w)
        rows = jnp.concatenate([near[0, :, at] + now[:, at]] + [a[:, at] for a in arrived], axis=0)
        part = prints[n][:, pl.ds(start, w)]
        scores += lax.dot_general(rows, part, (((1,), (1,)), ((), ())), preferred_element_type=jnp.float32)
    entry_sums = jnp.sum(jnp.where(select, scores, 0.0), axis=0, keepdims=True)
    coef = ((spread_by(entry_sums, same, 0) - measured) * certain).astype(jnp.bfloat16).astype(jnp.float32)
    spread = jnp.where(select, coef, 0.0).astype(jnp.bfloat16)
    for n, start, w in pieces:
        at = pl.ds(n * width + start, w)
        back = jnp.dot(spread, prints[n][:, pl.ds(start, w)], preferred_element_type=jnp.float32).astype(jnp.bfloat16)
        for p in range(owners):
            adjoint[p][:, at] = back[p * capacity : (p + 1) * capacity]
    modeled[...] = spread_by(entry_sums, member, 0)


def placing_kernel(*refs):
    placing, near, far, returned, (out, held, sems) = refs[0], refs[1], refs[2], refs[3:-3], refs[-3:]
    place = placing[...]
    copies = []
    for n, (start, width) in enumerate(chunks_of(held.shape[1], held.shape[1] // 8)):
        at = pl.ds(start, width)
        rows = [past[p, :, at] for past in (near, far) for p in range(past.shape[0])]
        rows = jnp.concatenate(rows + [r[:, at] for r in returned], axis=0)
        held[:, at] = lax.dot_general(place, rows, (((0,), (0,)), ((), ())), preferred_element_type=jnp.float32)
        copies.append(pltpu.make_async_copy(held.at[:, at], out.at[:, at], sems.at[n]))
        copies[-1].start()
    for copy in copies:
        copy.wait()


def on_device(flux, footprint, foot_slot, wanted, counts, observed, inv_var):
    steps_win, tiles_dev, cells = flux.shape
    owners = lax.axis_size("tile")
    capacity = wanted.shape[3]
    slots = owners * capacity
    own_rows = steps_win * tiles_dev
    soundings, per = foot_slot.shape[1:]
    entries = soundings * per
    half = functools.partial(jax.ShapeDtypeStruct, dtype=jnp.bfloat16)
    params = pltpu.CompilerParams

    table = wanted.reshape(owners, capacity).T
    base = lax.optimization_barrier(jnp.pad(table[None, None], ((0, 0), (0, 1), (0, 0), (0, 0))))
    ahead = passed_along(table, -1)
    tables = base + jnp.pad(ahead[None, None], ((0, 0), (1, 0), (0, 0), (0, 0)))
    while tables.shape[0] < owners:
        theirs = swapped(tables, tables.shape[0])
        tables = jnp.concatenate([tables, theirs])

    prints = footprint.reshape(soundings, per, cells)
    small = [foot_slot.reshape(soundings, per).T, counts.reshape(1, owners), observed, inv_var]
    part = (entries, cells // 2)
    first, *small = fetched([prints] + small, [part] + [x.shape for x in small], 0)
    (second,) = fetched([prints], [part], cells // 2)
    (own,) = fetched([flux.reshape(own_rows, cells)], [(own_rows, cells)], 0)

    block = half((capacity, cells))
    split = owners // 2
    gathered = pl.pallas_call(
        functools.partial(gather_kernel, owners, capacity),
        in_specs=[VMEM, VMEM],
        out_specs=[VMEM] * (owners + 3),
        out_shape=[half((owners - split, capacity, cells)), half((split, capacity, cells))]
        + [block] * owners
        + [half((2 * slots, own_rows))],
        compiler_params=params(vmem_limit_bytes=16 * MIB),
        name="gather",
    )(tables, own)
    far, near, now, placing = gathered[0], gathered[1], gathered[2:-1], gathered[-1]

    far = passed_along(far, 1)
    near = passed_along(near, 1)
    arrived = {}
    for p in [*range(split, owners), *range(1, split)]:
        past = near[p] if p < split else far[p - split]
        arrived[p] = swapped(past + now[p], p)
    arrived = [arrived[p] for p in range(1, owners)]

    results = pl.pallas_call(
        functools.partial(adjoint_kernel, owners, capacity, per),
        in_specs=[VMEM] * (7 + owners),
        out_specs=[VMEM] * (1 + owners),
        out_shape=[jax.ShapeDtypeStruct((1, soundings), jnp.float32)] + [block] * owners,
        compiler_params=params(vmem_limit_bytes=20 * MIB),
        name="adjoint",
    )(
        first,
        second,
        *small,
        near,
        now[0],
        *arrived,
    )
    modeled, adjoint = results[0], results[1:]

    returned = {0: adjoint[0]}
    for p in [*range(split, owners), *range(1, split)]:
        returned[p] = swapped(adjoint[p], p)
    returned = [returned[p] for p in range(owners)]
    near = passed_along(jnp.stack(returned[:split]), -1)
    far = passed_along(jnp.stack(returned[split:]), -1)

    grad = pl.pallas_call(
        placing_kernel,
        in_specs=[VMEM] * (3 + owners),
        out_specs=HBM,
        out_shape=jax.ShapeDtypeStruct((own_rows, cells), jnp.float32),
        scratch_shapes=[pltpu.VMEM((own_rows, cells), jnp.float32), pltpu.SemaphoreType.DMA((8,))],
        compiler_params=params(vmem_limit_bytes=20 * MIB),
        name="placing",
    )(placing, near, far, *returned)
    return (modeled, grad.reshape(steps_win, tiles_dev, cells))


def solution(mesh):
    placed = (
        P(("member", "tm"), "tile", None),
        P("tm", "tile", None, None),
        P("tm", "tile", None),
        P("tm", "tile", None, None),
        P("tm", "tile", None),
        P("tm", "tile"),
        P("tm", "tile"),
    )

    return jax.shard_map(
        on_device,
        mesh=mesh,
        in_specs=placed,
        out_specs=(P(("member", "tm"), "tile"), P(("member", "tm"), "tile", None)),
        check_vma=False,
    )
```

```python
import functools

import jax
import jax.numpy as jnp
from jax import lax
from jax.experimental import pallas as pl
from jax.experimental.pallas import tpu as pltpu
from jax.sharding import PartitionSpec as P


VMEM = pl.BlockSpec(memory_space=pltpu.VMEM)
HBM = pl.BlockSpec(memory_space=pltpu.HBM)
MIB = 1 << 20
PARTS = (1, 3, 4)


def passed_along(value, steps, ring):
    count = lax.axis_size("tm")
    sources = range(count) if ring else range(max(0, -steps), min(count, count - steps))
    return lax.ppermute(value, "tm", [(source, (source + steps) % count) for source in sources])


def swapped(value, mask):
    return lax.ppermute(value, "tile", [(j, j ^ mask) for j in range(lax.axis_size("tile"))])


def in_hbm(value):
    return pltpu.with_memory_space_constraint(value, pltpu.HBM)


def chunks_of(cells, width):
    width = min(width, cells)
    return [(start, width) for start in range(0, cells, width)]


def fetch_kernel(count, start, *refs):
    sources, kept, sems = refs[:count], refs[count : 2 * count], refs[2 * count]
    copies = []
    for n, (source, keep) in enumerate(zip(sources, kept)):
        if len(source.shape) == 3:
            soundings, per, cells = source.shape
            source = source.reshape(soundings * per, cells).at[:, pl.ds(start, keep.shape[1])]
        width = keep.shape[1]
        for m, (at, w) in enumerate(chunks_of(width, width // 4 if width % 4096 == 0 else width)):
            piece = pltpu.make_async_copy(source.at[:, pl.ds(at, w)], keep.at[:, pl.ds(at, w)], sems.at[n, m])
            piece.start()
            copies.append(piece)
    for copy in copies:
        copy.wait()


def fetched(sources, shapes, start):
    return pl.pallas_call(
        functools.partial(fetch_kernel, len(sources), start),
        in_specs=[HBM] * len(sources),
        out_specs=[VMEM] * len(sources),
        out_shape=[jax.ShapeDtypeStruct(shape, x.dtype) for shape, x in zip(shapes, sources)],
        scratch_shapes=[pltpu.SemaphoreType.DMA((len(sources), 4))],
        compiler_params=pltpu.CompilerParams(vmem_limit_bytes=12 * MIB),
    )(*[in_hbm(x) for x in sources])


def gather_kernel(owners, capacity, *refs):
    tables, own = refs[:2]
    later, now, placing = refs[2 : 2 + owners], refs[2 + owners : 2 + 2 * owners], refs[2 + 2 * owners]
    own_rows, cells = own.shape
    slots = owners * capacity
    last = lax.axis_index("tm") == lax.axis_size("tm") - 1
    asked = [tables[p, 1] for p in range(owners)] + [tables[p, 0] - own_rows for p in range(owners)]
    asked = jnp.concatenate(asked, axis=0)
    mine = lax.broadcasted_iota(jnp.int32, asked.shape, 1) == lax.axis_index("tile")
    ids = jnp.sum(jnp.where(mine, asked, 0), axis=1, keepdims=True)
    shape = (2 * slots, own_rows)
    ahead = lax.broadcasted_iota(jnp.int32, shape, 0) < jnp.where(last, slots, 0)
    place = one_if((ids == lax.broadcasted_iota(jnp.int32, shape, 1)) & jnp.logical_not(ahead))
    placing[...] = place
    for start, width in chunks_of(cells, cells // 4):
        at = pl.ds(start, width)
        rows = jnp.dot(place, own[:, at], preferred_element_type=jnp.float32).astype(jnp.bfloat16)
        for p in range(owners):
            later[p][:, at] = rows[p * capacity : (p + 1) * capacity]
            now[p][:, at] = rows[slots + p * capacity : slots + (p + 1) * capacity]


def in_parts(value):
    parts, rest = [], value
    for _ in range(3):
        parts.append(rest.astype(jnp.bfloat16).astype(jnp.float32))
        rest = rest - parts[-1]
    return jnp.concatenate(parts + [jnp.zeros((5, value.shape[1]), jnp.float32)], axis=0).astype(jnp.bfloat16)


def spread_by(value, picks, dim):
    parts = lax.dot_general(in_parts(value), picks, (((1,), (dim,)), ((), ())), preferred_element_type=jnp.float32)
    return parts[0:1] + parts[1:2] + parts[2:3]


def one_if(condition):
    return condition.astype(jnp.float32).astype(jnp.bfloat16)


def adjoint_kernel(owners, capacity, per, *refs):
    used, counts, observed, inv_var, past, now = refs[3:9]
    arrived = refs[9 : 8 + owners]
    modeled, adjoint = refs[8 + owners], refs[9 + owners : 9 + 2 * owners]
    third, sems = refs[9 + 2 * owners :]
    prints = refs[:2] + (third,)
    entries, cells = prints[0].shape[0], past.shape[1]
    unit = cells // 8
    rest = refs[2].reshape(entries, cells)
    copies = []
    for n, (start, w) in enumerate(chunks_of(third.shape[1], unit)):
        source = rest.at[:, pl.ds(cells - third.shape[1] + start, w)]
        copies.append(pltpu.make_async_copy(source, third.at[:, pl.ds(start, w)], sems.at[n]))
        copies[-1].start()
    soundings = entries // per
    slots = owners * capacity
    pieces = [(part, start, w) for part in prints for start, w in chunks_of(part.shape[1], unit)]
    shape = (entries, soundings)
    member = one_if(lax.broadcasted_iota(jnp.int32, shape, 0) // per == lax.broadcasted_iota(jnp.int32, shape, 1))
    shape = (entries, entries)
    same = one_if(lax.broadcasted_iota(jnp.int32, shape, 0) // per == lax.broadcasted_iota(jnp.int32, shape, 1) // per)
    measured = spread_by(observed[...], member, 1)
    certain = spread_by(inv_var[...], member, 1)
    entry = jnp.dot(used[...].astype(jnp.float32).astype(jnp.bfloat16), member.T, preferred_element_type=jnp.float32)
    own_entry = lax.broadcasted_iota(jnp.int32, (per, entries), 1) % per == lax.broadcasted_iota(jnp.int32, (per, entries), 0)
    entry = jnp.sum(jnp.where(own_entry, entry, 0.0), axis=0, keepdims=True).astype(jnp.int32)
    slot = lax.broadcasted_iota(jnp.int32, (slots, owners), 0)
    owner, place = (slot // capacity) ^ lax.axis_index("tile"), slot % capacity
    its = owner == lax.broadcasted_iota(jnp.int32, (slots, owners), 1)
    slot_of = jnp.where(its & (place < counts[...]), owner * capacity + place + 1, 0)
    slot_of = jnp.sum(slot_of, axis=1, keepdims=True) - 1
    select = entry == slot_of
    scores = jnp.zeros((slots, entries), jnp.float32)
    for n, (part, start, w) in enumerate(pieces):
        at = pl.ds(n * unit, unit)
        rows = jnp.concatenate([past[:, at] + now[:, at]] + [a[:, at] for a in arrived], axis=0)
        if part is third:
            copies[start // unit].wait()
        scores += lax.dot_general(rows, part[:, pl.ds(start, w)], (((1,), (1,)), ((), ())), preferred_element_type=jnp.float32)
    entry_sums = jnp.sum(jnp.where(select, scores, 0.0), axis=0, keepdims=True)
    coef = ((spread_by(entry_sums, same, 0) - measured) * certain).astype(jnp.bfloat16).astype(jnp.float32)
    spread = jnp.where(select, coef, 0.0).astype(jnp.bfloat16)
    for n, (part, start, w) in enumerate(pieces):
        at = pl.ds(n * unit, unit)
        back = jnp.dot(spread, part[:, pl.ds(start, w)], preferred_element_type=jnp.float32).astype(jnp.bfloat16)
        for p in range(owners):
            adjoint[p][:, at] = back[p * capacity : (p + 1) * capacity]
    modeled[...] = spread_by(entry_sums, member, 0)


def placing_kernel(*refs):
    placing, returned, (out, held, sems) = refs[0], refs[1:-3], refs[-3:]
    place = placing[...]
    copies = []
    for n, (start, width) in enumerate(chunks_of(held.shape[1], held.shape[1] // 8)):
        at = pl.ds(start, width)
        rows = jnp.concatenate([r[:, at] for r in returned], axis=0)
        held[:, at] = lax.dot_general(place, rows, (((0,), (0,)), ((), ())), preferred_element_type=jnp.float32)
        copies.append(pltpu.make_async_copy(held.at[:, at], out.at[:, at], sems.at[n]))
        copies[-1].start()
    for copy in copies:
        copy.wait()


def on_device(flux, footprint, foot_slot, wanted, counts, observed, inv_var):
    steps_win, tiles_dev, cells = flux.shape
    owners = lax.axis_size("tile")
    capacity = wanted.shape[3]
    slots = owners * capacity
    own_rows = steps_win * tiles_dev
    soundings, per = foot_slot.shape[1:]
    entries = soundings * per
    half = functools.partial(jax.ShapeDtypeStruct, dtype=jnp.bfloat16)
    params = pltpu.CompilerParams

    table = wanted.reshape(owners, capacity).T
    ahead = passed_along(table, -1, False)
    prints = footprint.reshape(soundings, per, cells)
    unit = cells // 8
    own = flux.reshape(own_rows, cells)
    small = [table, foot_slot.reshape(soundings, per).T, counts.reshape(1, owners), observed, inv_var]
    shapes = [(entries, PARTS[0] * unit), own.shape] + [x.shape for x in small]
    first, own, table, *small = fetched([prints, own] + small, shapes, 0)
    (second,) = fetched([prints], [(entries, PARTS[1] * unit)], PARTS[0] * unit)
    tables = jnp.stack([table, ahead])[None]
    while tables.shape[0] < owners:
        theirs = swapped(tables, tables.shape[0])
        tables = jnp.concatenate([tables, theirs])

    block = half((capacity, cells))
    gathered = pl.pallas_call(
        functools.partial(gather_kernel, owners, capacity),
        in_specs=[VMEM, VMEM],
        out_specs=[VMEM] * (2 * owners + 1),
        out_shape=[block] * (2 * owners) + [half((2 * slots, own_rows))],
        compiler_params=params(vmem_limit_bytes=16 * MIB),
        name="gather",
    )(tables, own)
    later, now, placing = gathered[:owners], gathered[owners:-1], gathered[-1]

    past, arrived = [None] * owners, [None] * owners
    for p in reversed(range(owners)):
        past[p] = passed_along(later[p], 1, True)
    for p in reversed(range(1, owners)):
        arrived[p] = swapped(past[p] + now[p], p)
    arrived = arrived[1:]

    results = pl.pallas_call(
        functools.partial(adjoint_kernel, owners, capacity, per),
        in_specs=[VMEM, VMEM, HBM] + [VMEM] * (5 + owners),
        out_specs=[VMEM] * (1 + owners),
        out_shape=[jax.ShapeDtypeStruct((1, soundings), jnp.float32)] + [block] * owners,
        scratch_shapes=[pltpu.VMEM((entries, PARTS[2] * unit), jnp.bfloat16), pltpu.SemaphoreType.DMA((PARTS[2],))],
        compiler_params=params(vmem_limit_bytes=20 * MIB),
        name="adjoint",
    )(
        first,
        second,
        in_hbm(prints),
        *small,
        past[0],
        now[0],
        *arrived,
    )
    modeled, adjoint = results[0], results[1:]

    returned, incoming = [adjoint[0]] + [None] * (owners - 1), [None] * owners
    for p in reversed(range(1, owners)):
        returned[p] = swapped(adjoint[p], p)
    for p in range(owners):
        incoming[p] = passed_along(returned[p], -1, True)

    grad = pl.pallas_call(
        placing_kernel,
        in_specs=[VMEM] * (1 + 2 * owners),
        out_specs=HBM,
        out_shape=jax.ShapeDtypeStruct((own_rows, cells), jnp.float32),
        scratch_shapes=[pltpu.VMEM((own_rows, cells), jnp.float32), pltpu.SemaphoreType.DMA((8,))],
        compiler_params=params(vmem_limit_bytes=20 * MIB),
        name="placing",
    )(placing, *incoming, *returned)
    return (modeled, grad.reshape(steps_win, tiles_dev, cells))


def solution(mesh):
    placed = (
        P(("member", "tm"), "tile", None),
        P("tm", "tile", None, None),
        P("tm", "tile", None),
        P("tm", "tile", None, None),
        P("tm", "tile", None),
        P("tm", "tile"),
        P("tm", "tile"),
    )

    return jax.shard_map(
        on_device,
        mesh=mesh,
        in_specs=placed,
        out_specs=(P(("member", "tm"), "tile"), P(("member", "tm"), "tile", None)),
        check_vma=False,
    )
```
